32 devices in a mesh: section: 4 (over x, core), blk: 4 (over z), tp: 2 (over y).
Axes of the slice: x: 2, y: 2, z: 4, core: 2. Of those that a mesh axis runs over, the one named last changes fastest.
Arguments:
- query: bfloat16 [2048, 8192], P(('section', 'blk'), 'tp'), may hold values from -6 to 6
- text_frame: int32 [2048], P(('section', 'blk')), may hold values from 0 to 63
- image_feats: bfloat16 [1024, 8192], P('blk', ('section', 'tp')), may hold values from -6 to 6
- image_frame: int32 [1024], P('blk'), may hold values from 0 to 63, never falling along the last dimension, each value on 1 to 32 neighbouring positions
- kv_weight: bfloat16 [4, 8192, 2, 1024], P('section', None, None, 'tp'), may hold values from -0.0625 to 0.0625
- query_gain: float32 [4, 128], P('section'), may hold values from 0.1 to 1.9
- key_gain: float32 [4, 128], P('section'), may hold values from 0.1 to 1.9
Outputs:
- attended: bfloat16 [2048, 8192], P(('section', 'blk'), 'tp')
The draws below stay inside these ranges and needn't reach their ends.
Inputs may be any that keep to these rules, and one draw needn't show every extreme that they name: `image_frame`: image frame ids never fall along the image tokens; every frame has at least one token.
All inputs are finite; a program needn't handle non-finite values.
Results may differ from the reference program's by a relative error of at most 0.007.
Values may be sent and summed in bfloat16 or wider, within the bound.
A program may use at most 128 MiB of HBM per device.

```python
import math
import jax
import jax.numpy as jnp
import numpy as np
from jax import lax

HEADS = 64
KV_HEADS = 8
HEAD = 128
VW = 8192
FRAMES = 64
IMG = 1024
TEXT = 2048
SECTIONS = 4
N_SECTION = 4


def set_ends(entries, stream_key, low, largest):
    dims = entries.shape
    spot = [jax.random.randint(jax.random.fold_in(stream_key, axis), (), 0, dims[axis]) for axis in range(len(dims))]
    entries = entries.at[tuple(spot)].set(low)
    longest = dims.index(max(dims))
    spot[longest] = (spot[longest] + 1) % dims[longest]
    return entries.at[tuple(spot)].set(largest)


def steps_of(stream_key, dims, split, low, largest):
    def one(position, blocks):
        draws = jax.random.uniform(jax.random.fold_in(jax.random.fold_in(stream_key, 6), position), (blocks,), jnp.float32, low / len(split), largest / len(split))
        return jnp.repeat(jnp.exp(draws), dims[position] // blocks).reshape((-1,) + (1,) * (len(dims) - position - 1))

    factor_of = one(*split[0])
    for cut in split[1:]:
        factor_of = factor_of * one(*cut)
    return factor_of


def length_profile(count, total, reach, slope):
    weights = [(1 << 20) // math.isqrt(standing ** slope) + 1 for standing in range(2, count + 1)]
    spare, counts = total - reach - (count - 1), [1] * (count - 1)
    while spare > 0:
        free = [i for i in range(count - 1) if counts[i] < reach]
        whole, budget = sum([weights[i] for i in free]), spare
        for i in free:
            extra = min(reach - counts[i], max(1, budget * weights[i] // whole), spare)
            counts[i] = counts[i] + extra
            spare = spare - extra
    return np.array([reach] + counts)


def ragged_sizes(key, count, total, bound, skew):
    if count == 2:
        one = jax.random.randint(key, (), max(1, total - bound), min(bound, total - 1) + 1)
        return jnp.stack([one, total - one])
    lengths = jnp.asarray(length_profile(count, total, bound, skew), jnp.int32)
    pairs = (count - 1) // 2
    donor, taker = lengths[1:1 + 2 * pairs:2], lengths[2:2 + 2 * pairs:2]
    room = jnp.minimum(donor - 1, bound - taker)
    shifted = jax.random.randint(jax.random.fold_in(key, 1), (pairs,), 0, 1 << 20) % (room + 1)
    lengths = lengths.at[1:1 + 2 * pairs:2].set(donor - shifted).at[2:2 + 2 * pairs:2].set(taker + shifted)
    return lengths[jax.random.permutation(jax.random.fold_in(key, 2), count)]


def centred(rng, dims, deviation, limit, shards=(), kind=jnp.bfloat16):
    entries = jax.random.normal(rng, dims, jnp.float32) * deviation
    if len(shards) > 0:
        entries = steps_of(rng, dims, shards, -0.22, 0.18) * entries
    return jnp.clip(entries, min=-limit, max=limit).astype(kind)


def setup_inputs(seed: int = 0) -> dict:
    key_of = jax.random.split(jax.random.key(seed), 8)
    query = centred(key_of[0], (TEXT, HEADS * HEAD), 1.0, 6.0, ((0, 16), (1, 2)))
    text_frame = set_ends(jax.random.randint(key_of[1], (TEXT,), 0, FRAMES), jax.random.fold_in(key_of[1], 1), 0, FRAMES - 1).astype(jnp.int32)
    image_feats = centred(key_of[2], (IMG, VW), 1.0, 6.0, ((0, 4), (1, 8)))
    image_frame = jnp.searchsorted(jnp.cumsum(ragged_sizes(key_of[3], FRAMES, IMG, 2 * IMG // FRAMES, 0)), jnp.arange(IMG), side="right").astype(jnp.int32)
    kv_weight = centred(key_of[4], (SECTIONS, VW, 2, KV_HEADS * HEAD), VW ** -0.5, 0.0625, ((0, 4), (3, 2)))
    query_gain = jnp.clip(1.0 + 0.18 * jax.random.normal(key_of[5], (SECTIONS, HEAD), jnp.float32), 0.1, 1.9)
    key_gain = jnp.clip(1.0 + 0.18 * jax.random.normal(key_of[6], (SECTIONS, HEAD), jnp.float32), 0.1, 1.9)
    return dict(query=query, text_frame=text_frame, image_feats=image_feats, image_frame=image_frame, kv_weight=kv_weight, query_gain=query_gain, key_gain=key_gain)


def normalize(x):
    return x * lax.rsqrt(lax.optimization_barrier(jnp.mean(x * x, axis=-1, keepdims=True)) + 1e-05)

def one_head(q, k, v, allowed):
    scores = jnp.einsum('tgd,sd->gts', q.astype(jnp.float32), k.astype(jnp.float32))
    weights = jnp.where(allowed[None], jnp.exp(scores), jnp.float32(0.0))
    total = lax.optimization_barrier(jnp.sum(weights, axis=-1, keepdims=True))
    wb = weights.astype(jnp.bfloat16)
    summed = jnp.einsum('gts,sd->gtd', wb.astype(jnp.float32), v.astype(jnp.float32))
    return summed / total

def reference(query, text_frame, image_feats, image_frame, kv_weight, query_gain, key_gain):
    rows = TEXT // N_SECTION
    groups = HEADS // KV_HEADS
    outputs = []
    for section_id in range(N_SECTION):
        weight = kv_weight[section_id].reshape(VW, 2 * KV_HEADS * HEAD)
        proj = jnp.dot(image_feats, weight, preferred_element_type=jnp.float32).reshape(IMG, 2, KV_HEADS, HEAD)
        keys = (normalize(proj[:, 0]) * key_gain[section_id]).astype(jnp.bfloat16)
        values = proj[:, 1].astype(jnp.bfloat16)
        qrows = query[section_id * rows:(section_id + 1) * rows].astype(jnp.float32).reshape(rows, KV_HEADS, groups, HEAD)
        qn = (normalize(qrows) * query_gain[section_id] * HEAD ** (-0.5)).astype(jnp.bfloat16)
        frames = text_frame[section_id * rows:(section_id + 1) * rows]
        allowed = image_frame[None, :] <= frames[:, None]
        result = lax.map(lambda item: one_head(item[0], item[1], item[2], allowed), (qn.transpose(1, 0, 2, 3), keys.transpose(1, 0, 2), values.transpose(1, 0, 2)))
        outputs.append(result.transpose(2, 0, 1, 3).reshape(rows, HEADS * HEAD).astype(jnp.bfloat16))
    return jnp.concatenate(outputs, axis=0)
```

```python
import functools

import jax
import jax.numpy as jnp
from jax import lax
from jax.experimental import pallas as pl
from jax.experimental.pallas import tpu as pltpu
from jax.sharding import PartitionSpec as P

MESH = pl.DeviceIdType.MESH
BF16 = jnp.bfloat16
F32 = jnp.float32
EPS = 1e-05


def kernel(
    dims,
    q_ref, tf_ref, x_ref, fr_ref, w_ref, qg_ref, kg_ref,
    out_ref,
    stage, kvw, xg, kv, frames, qn, acc, tot, proj,
    wsem, fsend, frecv, ssend, srecv, rsend, rrecv, zsend, zrecv,
):
    n_sec, n_blk, n_tp, n_chunk, w_rows = dims
    sec, blk, tp = lax.axis_index("section"), lax.axis_index("blk"), lax.axis_index("tp")
    par = lax.rem(sec, 2)
    half = sec // 2
    mine = half * n_tp + tp
    n_half = n_sec // 2
    n_group = n_half * n_tp
    rows, fw = x_ref.shape
    rc = rows // n_chunk
    feats, _, kv_cols = w_ref.shape[1:]
    head = qg_ref.shape[1]
    heads_kv = kv_cols // head
    text = q_ref.shape[0]
    groups = q_ref.shape[1] // kv_cols
    n_w = feats // w_rows
    n_stage = stage.shape[0]
    sibling = {"section": sec + 1 - 2 * par}

    def w_copy(i):
        return pltpu.make_async_copy(
            w_ref.at[0, pl.ds(i * w_rows, w_rows)], stage.at[i % n_stage], wsem.at[i % n_stage]
        )

    for i in range(min(n_stage, n_w)):
        w_copy(i).start()

    def plane_peer(k):
        other = lax.rem(mine + k, n_group)
        return {"section": 2 * (other // n_tp) + par, "tp": lax.rem(other, n_tp)}

    def line_peer(k):
        return {"blk": lax.rem(blk + k, n_blk)}

    barrier = pltpu.get_barrier_semaphore()
    pl.semaphore_signal(barrier, inc=1, device_id=sibling, device_id_type=MESH)
    for k in range(1, n_group):
        pl.semaphore_signal(barrier, inc=1, device_id=plane_peer(k), device_id_type=MESH)
    for k in range(1, n_blk):
        pl.semaphore_signal(barrier, inc=1, device_id=line_peer(k), device_id_type=MESH)
    pl.semaphore_wait(barrier, n_group + n_blk - 1)

    square = n_half == 2 and n_tp == 2
    near = ({"section": 2 * (1 - half) + par}, {"tp": 1 - tp})
    near_at = ((1 - half) * n_tp + tp, half * n_tp + 1 - tp)

    def feature_copy(c, k):
        return pltpu.make_async_remote_copy(
            src_ref=x_ref.at[pl.ds(c * rc, rc)],
            dst_ref=xg.at[c, par, mine],
            send_sem=fsend.at[c, k if square else 0],
            recv_sem=frecv.at[c, k if square else 2],
            device_id=near[k] if square else plane_peer(k),
            device_id_type=MESH,
        )

    def arrived(c, k):
        return pltpu.make_async_remote_copy(
            src_ref=x_ref.at[pl.ds(c * rc, rc)],
            dst_ref=xg.at[c, par, near_at[k]],
            send_sem=fsend.at[c, k],
            recv_sem=frecv.at[c, k],
            device_id=near[k],
            device_id_type=MESH,
        )

    def corner_copy(c, k, at):
        part = xg.at[c, par, at, pl.ds(k * (rc // 2), rc // 2)]
        return pltpu.make_async_remote_copy(
            src_ref=part,
            dst_ref=part,
            send_sem=fsend.at[c, 2 + k],
            recv_sem=frecv.at[c, 3 + k],
            device_id=near[1 - k],
            device_id_type=MESH,
        )

    def local_copy(c):
        return pltpu.make_async_copy(
            x_ref.at[pl.ds(c * rc, rc)], xg.at[c, par, mine], frecv.at[c, 2]
        )

    def start(c):
        for k in range(2) if square else range(1, n_group):
            feature_copy(c, k).start()
        local_copy(c).start()

    def forward(c):
        if square:
            for k in range(2):
                arrived(c, k).wait_recv()
                corner_copy(c, k, near_at[k]).start()

    start(0)
    if n_chunk > 1:
        start(1)

    def frame_copy(k):
        return pltpu.make_async_remote_copy(
            src_ref=fr_ref,
            dst_ref=frames.at[blk],
            send_sem=rsend,
            recv_sem=rrecv,
            device_id=line_peer(k),
            device_id_type=MESH,
        )

    pltpu.make_async_copy(fr_ref, frames.at[blk], rrecv).start()
    for k in range(1, n_blk):
        frame_copy(k).start()

    def share(c):
        return pltpu.make_async_remote_copy(
            src_ref=xg.at[c, par],
            dst_ref=xg.at[c, par],
            send_sem=ssend.at[c],
            recv_sem=srecv.at[c],
            device_id=sibling,
            device_id_type=MESH,
        )

    def pass_on(c):
        if square:
            local_copy(c).wait()
            for k in range(2):
                corner_copy(c, k, (1 - half) * n_tp + 1 - tp).wait_recv()
        else:
            pltpu.make_async_copy(xg.at[c, par], xg.at[c, par], frecv.at[c, 2]).wait()
        share(c).start()

    sub = 2 * head
    ri = lax.broadcasted_iota(jnp.int32, (sub, sub), 0)
    ci = lax.broadcasted_iota(jnp.int32, (sub, sub), 1)
    take = (ci == 2 * lax.rem(ri, head) + ri // head).astype(BF16)
    for i in range(n_w):
        w_copy(i).wait()

        @pl.loop(0, w_rows // head, unroll=4)
        def _(j):
            at = pl.multiple_of(j * head, head)
            block = stage[i % n_stage, pl.ds(at, head)].reshape(sub, kv_cols)
            apart = jnp.dot(take, block, preferred_element_type=F32).astype(BF16)
            to = pl.multiple_of(i * w_rows + j * head, head)
            kvw[pl.ds(to, head), :kv_cols] = apart[:head]
            kvw[pl.ds(to, head), kv_cols:] = apart[head:]

        if i + n_stage < n_w:
            w_copy(i + n_stage).start()
        if i == n_w // 8:
            forward(0)
            if n_chunk > 2:
                start(2)
        if i == (3 * n_w) // 8:
            pass_on(0)
        if i == (5 * n_w) // 8 and n_chunk > 1:
            forward(1)
            if n_chunk > 3:
                start(3)

    def line_copy(way, src, d, c):
        to = blk + 1 if way == 0 else blk - 1
        return pltpu.make_async_remote_copy(
            src_ref=kv.at[src, c],
            dst_ref=kv.at[src, c],
            send_sem=zsend.at[way, d - 1, c],
            recv_sem=zrecv.at[way, d - 1, c],
            device_id={"blk": to},
            device_id_type=MESH,
        )

    can = (blk + 1 < n_blk, blk >= 1)

    def source(way, d):
        return blk - d if way == 0 else blk + d

    def exists(way, d):
        return blk - d >= 0 if way == 0 else blk + d < n_blk

    def relay(way, d, c):
        @pl.when(exists(way, d))
        def _():
            src = source(way, d)
            line_copy(way, src, d, c).wait_recv()

            @pl.when(can[way])
            def _():
                line_copy(way, src, d + 1, c).start()

    for c in range(n_chunk):
        share(c).wait_recv()
        proj[...] = jnp.zeros_like(proj)

        @pl.loop(0, n_group, unroll=2)
        def _(j):
            for p in range(2):
                place = ((2 * (j // n_tp) + p) * n_tp + lax.rem(j, n_tp)) * fw
                part = kvw[pl.ds(pl.multiple_of(place, fw), fw), :]
                proj[...] += jnp.dot(xg[c, p, j], part, preferred_element_type=F32)

        for h in range(heads_kv):
            key = proj[:, h * head:(h + 1) * head]
            scale = lax.rsqrt(jnp.mean(key * key, axis=-1, keepdims=True) + EPS)
            kv[blk, c, :, h * head:(h + 1) * head] = (key * scale * kg_ref[...]).astype(BF16)
        kv[blk, c, :, kv_cols:] = proj[:, kv_cols:].astype(BF16)
        for way in range(2):
            @pl.when(can[way])
            def _():
                line_copy(way, blk, 1, c).start()
        if c + 1 < n_chunk:
            pass_on(c + 1)
        if c >= 1:
            for way in range(2):
                relay(way, 1, c - 1)
        if c + 2 < n_chunk:
            forward(c + 2)
        if c + 4 < n_chunk:
            start(c + 4)

    gain = qg_ref[...] * head ** (-0.5)

    @pl.loop(0, heads_kv)
    def _(k):
        for g in range(groups):
            col = pl.multiple_of((k * groups + g) * head, head)
            rowsq = q_ref[:, pl.ds(col, head)].astype(F32)
            scale = lax.rsqrt(jnp.mean(rowsq * rowsq, axis=-1, keepdims=True) + EPS)
            qn[k, g * text:(g + 1) * text, :] = (rowsq * scale * gain).astype(BF16)

    pltpu.make_async_copy(frames, frames, rrecv).wait()
    limit = jnp.broadcast_to(tf_ref[...], (text, text)).T[:, :1]
    acc[...] = jnp.zeros_like(acc)
    tot[...] = jnp.zeros_like(tot)

    def attend(src):
        allowed = frames[src] <= limit

        @pl.loop(0, heads_kv)
        def _(k):
            at = pl.multiple_of(k * head, head)
            keys = kv[src, :, :, pl.ds(at, head)].reshape(rows, head)
            values = kv[src, :, :, pl.ds(kv_cols + at, head)].reshape(rows, head)
            for g in range(groups):
                span = slice(g * text, (g + 1) * text)
                scores = lax.dot_general(
                    qn[k, span, :], keys, (((1,), (1,)), ((), ())), preferred_element_type=F32
                )
                weights = jnp.where(allowed, jnp.exp(scores), 0.0)
                total = weights[:, :head]
                for m in range(1, rows // head):
                    total = total + weights[:, m * head:(m + 1) * head]
                tot[k, span, :] += total
                acc[k, span, :] += jnp.dot(
                    weights.astype(BF16), values, preferred_element_type=F32
                )

    def attend_if(way, d):
        @pl.when(exists(way, d))
        def _():
            attend(source(way, d))

    for way in range(2):
        relay(way, 1, n_chunk - 1)
    attend(blk)

    @pl.loop(1, n_blk - 1)
    def _(d):
        for c in range(n_chunk):
            for way in range(2):
                relay(way, d + 1, c)
            if c < 2:
                attend_if(c, d)

    for way in range(2):
        attend_if(way, n_blk - 1)

    @pl.loop(0, heads_kv)
    def _(k):
        for g in range(groups):
            span = slice(g * text, (g + 1) * text)
            total = jnp.sum(tot[k, span, :], axis=-1, keepdims=True)
            col = pl.multiple_of((k * groups + g) * head, head)
            out_ref[:, pl.ds(col, head)] = (acc[k, span, :] / total).astype(BF16)

    for c in range(n_chunk):
        if square:
            for k in range(2):
                feature_copy(c, k).wait_send()
                corner_copy(c, k, near_at[k]).wait_send()
        elif n_group > 1:
            gone = xg.at[c, par, pl.ds(0, n_group - 1)]
            pltpu.make_async_copy(gone, gone, fsend.at[c, 0]).wait()
        share(c).wait_send()
    if n_blk > 1:
        gone = frames.at[pl.ds(0, n_blk - 1)]
        pltpu.make_async_copy(gone, gone, rsend).wait()

    @pl.loop(1, n_blk)
    def _(d):
        for way in range(2):
            @pl.when(can[way] & exists(way, d - 1))
            def _():
                for c in range(n_chunk):
                    line_copy(way, source(way, d - 1), d, c).wait_send()


def plane_kernel(
    dims,
    q_ref, tf_ref, x_ref, fr_ref, w_ref, qg_ref, kg_ref,
    out_ref,
    raw, kvw, xg, kv, frames, qv, qn, proj, outv,
    wsem, qsem, osem, lsem, nsend, nrecv, csend, crecv, ssend, srecv,
    rsend, rrecv, zsend, zrecv,
):
    n_sec, n_blk, n_tp, n_chunk = dims
    sec, blk, tp = lax.axis_index("section"), lax.axis_index("blk"), lax.axis_index("tp")
    par = lax.rem(sec, 2)
    half = sec // 2
    rows, fw = x_ref.shape
    rc = rows // n_chunk
    feats, _, kv_cols = w_ref.shape[1:]
    head = qg_ref.shape[1]
    heads_kv = kv_cols // head
    text = qv.shape[0]
    groups = qv.shape[1] // kv_cols
    n_slice = feats // fw
    last = n_blk - 1

    mine = half * n_tp + tp
    near = ({"section": 2 * (1 - half) + par}, {"tp": 1 - tp})
    near_at = ((1 - half) * n_tp + tp, half * n_tp + 1 - tp)
    corner_at = (1 - half) * n_tp + 1 - tp
    slots = (mine, near_at[0], near_at[1], corner_at)
    sibling = {"section": sec + 1 - 2 * par}

    def x_copy(c):
        return pltpu.make_async_copy(
            x_ref.at[pl.ds(c * rc, rc)], xg.at[c, par, mine], lsem.at[c]
        )

    def w_copy(i):
        span = pl.ds(i * fw, fw)
        return pltpu.make_async_copy(w_ref.at[0, span], raw.at[span], wsem.at[i])

    q_copy = pltpu.make_async_copy(q_ref, qv, qsem)
    for c in range(n_chunk):
        x_copy(c).start()
    for i in range(n_slice):
        w_copy(i).start()
    q_copy.start()

    def line_peer(k):
        return {"blk": lax.rem(blk + k, n_blk)}

    barrier = pltpu.get_barrier_semaphore()
    for peer in (sibling, near[0], near[1]):
        pl.semaphore_signal(barrier, inc=1, device_id=peer, device_id_type=MESH)
    for k in range(1, n_blk):
        pl.semaphore_signal(barrier, inc=1, device_id=line_peer(k), device_id_type=MESH)
    pl.semaphore_wait(barrier, n_blk + 2)

    def near_copy(c, k, at):
        return pltpu.make_async_remote_copy(
            src_ref=xg.at[c, par, at],
            dst_ref=xg.at[c, par, at],
            send_sem=nsend.at[c, k],
            recv_sem=nrecv.at[c, k],
            device_id=near[k],
            device_id_type=MESH,
        )

    def corner_copy(c, k, at):
        part = xg.at[c, par, at, pl.ds(k * (rc // 2), rc // 2)]
        return pltpu.make_async_remote_copy(
            src_ref=part,
            dst_ref=part,
            send_sem=csend.at[c, k],
            recv_sem=crecv.at[c, k],
            device_id=near[1 - k],
            device_id_type=MESH,
        )

    def share(c, i, side):
        return pltpu.make_async_remote_copy(
            src_ref=xg.at[c, side, slots[i]],
            dst_ref=xg.at[c, side, slots[i]],
            send_sem=ssend.at[c, i],
            recv_sem=srecv.at[c, i],
            device_id=sibling,
            device_id_type=MESH,
        )

    def start(c):
        x_copy(c).wait()
        for k in range(2):
            near_copy(c, k, mine).start()
        share(c, 0, par).start()

    def forward(c):
        for k in range(2):
            near_copy(c, k, near_at[k]).wait_recv()
            corner_copy(c, k, near_at[k]).start()
            share(c, 1 + k, par).start()
        if c + 1 < n_chunk:
            start(c + 1)

    def turn(c):
        for k in range(2):
            corner_copy(c, k, corner_at).wait_recv()
        share(c, 3, par).start()

    def frame_copy(k):
        return pltpu.make_async_remote_copy(
            src_ref=fr_ref,
            dst_ref=frames.at[blk],
            send_sem=rsend,
            recv_sem=rrecv,
            device_id=line_peer(k),
            device_id_type=MESH,
        )

    start(0)
    pltpu.make_async_copy(fr_ref, frames.at[blk], rrecv).start()
    for k in range(1, n_blk):
        frame_copy(k).start()

    part = fw // 2
    for i in range(n_slice):
        w_copy(i).wait()

        @pl.loop(0, fw // part, unroll=2)
        def _(j):
            span = pl.ds(pl.multiple_of(i * fw + j * part, part), part)
            kvw[span, :] = raw[span].reshape(part, 2 * kv_cols)

        if i == n_slice - 2:
            forward(0)

    def along(way):
        return blk if way == 0 else last - blk

    def at(way, u):
        return u if way == 0 else last - u

    def line_copy(way, kind, src, to, c, by_head):
        piece = kv.at[src, c] if by_head else kv.at[src, :, pl.ds(c * rc, rc)]
        return pltpu.make_async_remote_copy(
            src_ref=piece,
            dst_ref=piece,
            send_sem=zsend.at[way, kind, c],
            recv_sem=zrecv.at[way, src, c],
            device_id={"blk": to},
            device_id_type=MESH,
        )

    def hop(way, c):
        u = along(way)
        return line_copy(way, 0, blk, at(way, u + 1), c, False)

    def leap(way, c):
        return line_copy(way, 1, blk, at(way, 2), c, False)

    def send(c):
        for way in range(2):
            u = along(way)

            @pl.when(u == 0)
            def _():
                leap(way, c).start()

            @pl.when(u < last)
            def _():
                hop(way, c).start()

    def relay_copy(way, c, first):
        return line_copy(way, 2 if first else 3, at(way, 1 if first else 0), at(way, last), c, not first)

    def arrived(way, u, c, by_head):
        line_copy(way, 0, at(way, u), blk, c, by_head).wait_recv()

    def relay(c):
        for way in range(2):
            @pl.when(along(way) == 2)
            def _():
                arrived(way, 1, c, False)
                relay_copy(way, c, True).start()

    def add(c, i):
        for p in range(2):
            place = ((2 * (slots[i] // n_tp) + p) * n_tp + lax.rem(slots[i], n_tp)) * fw
            weight = kvw[pl.ds(pl.multiple_of(place, fw), fw), :]
            proj[...] += jnp.dot(xg[c, p, slots[i]], weight, preferred_element_type=F32)

    for c in range(n_chunk):
        proj[...] = jnp.zeros_like(proj)
        share(c, 0, 1 - par).wait_recv()
        add(c, 0)
        if c >= 1:
            forward(c)
        if c >= 2:
            relay(c - 2)
        for i in (1, 2):
            share(c, i, 1 - par).wait_recv()
            add(c, i)
        turn(c)
        share(c, 3, 1 - par).wait_recv()
        add(c, 3)
        for h in range(heads_kv):
            key = proj[:, h * head:(h + 1) * head]
            scale = lax.rsqrt(jnp.mean(key * key, axis=-1, keepdims=True) + EPS)
            kv[blk, h, c * rc:(c + 1) * rc, :head] = (key * scale * kg_ref[...]).astype(BF16)
            kv[blk, h, c * rc:(c + 1) * rc, head:] = (
                proj[:, kv_cols + h * head:kv_cols + (h + 1) * head].astype(BF16)
            )
        send(c)

    relay(n_chunk - 2)
    relay(n_chunk - 1)

    for way in range(2):
        @pl.when(along(way) == 2)
        def _():
            for c in range(n_chunk):
                arrived(way, 0, c, False)
            for h in range(heads_kv):
                relay_copy(way, h, False).start()

    q_copy.wait()
    gain = qg_ref[...] * head ** (-0.5)

    @pl.loop(0, heads_kv)
    def _(k):
        for g in range(groups):
            col = pl.multiple_of((k * groups + g) * head, head)
            rowsq = qv[:, pl.ds(col, head)].astype(F32)
            scale = lax.rsqrt(jnp.mean(rowsq * rowsq, axis=-1, keepdims=True) + EPS)
            qn[k, g * text:(g + 1) * text, :] = (rowsq * scale * gain).astype(BF16)

    pltpu.make_async_copy(frames, frames, rrecv).wait()
    limit = jnp.broadcast_to(tf_ref[...], (text, text)).T[:, :1]
    allowed = jnp.concatenate([frames[s] for s in range(n_blk)], axis=1) <= limit

    for way in range(2):
        for u in (0, 1, 2):
            if u < 2:
                @pl.when(along(way) == u + 1)
                def _():
                    if u == 0:
                        for c in range(n_chunk):
                            arrived(way, 0, c, False)

            @pl.when(along(way) == last)
            def _():
                if u > 0:
                    for c in range(n_chunk):
                        arrived(way, u, c, False)

    def out_copy(k):
        return pltpu.make_async_copy(
            outv.at[k], out_ref.at[:, pl.ds(pl.multiple_of(k * groups * head, head), groups * head)], osem.at[k]
        )

    @pl.loop(0, heads_kv)
    def _(k):
        for way in range(2):
            @pl.when(along(way) == last)
            def _():
                arrived(way, 0, k, True)

        keys = jnp.concatenate([kv[s, k, :, :head] for s in range(n_blk)], axis=0)
        values = jnp.concatenate([kv[s, k, :, head:] for s in range(n_blk)], axis=0)
        n_rows = groups * text
        scores = lax.dot_general(
            qn[k], keys, (((1,), (1,)), ((), ())), preferred_element_type=F32
        )
        weights = jnp.where(
            allowed[None], jnp.exp(scores).reshape(groups, text, n_blk * rows), 0.0
        ).reshape(n_rows, n_blk * rows)
        total = weights[:, :head]
        for m in range(1, n_blk * rows // head):
            total = total + weights[:, m * head:(m + 1) * head]
        total = jnp.sum(total, axis=-1, keepdims=True)
        result = jnp.dot(weights.astype(BF16), values, preferred_element_type=F32)
        result = (result / total).astype(BF16)
        for g in range(groups):
            outv[k, :, g * head:(g + 1) * head] = result[g * text:(g + 1) * text]
        out_copy(k).start()

    for c in range(n_chunk):
        for k in range(2):
            near_copy(c, k, mine).wait_send()
            corner_copy(c, k, near_at[k]).wait_send()
        for i in range(4):
            share(c, i, par).wait_send()
    gone = frames.at[pl.ds(0, n_blk - 1)]
    pltpu.make_async_copy(gone, gone, rsend).wait()
    for way in range(2):
        u = along(way)
        for c in range(n_chunk):
            @pl.when(u < last)
            def _():
                hop(way, c).wait_send()

            @pl.when(u == 0)
            def _():
                leap(way, c).wait_send()

            @pl.when(u == 2)
            def _():
                relay_copy(way, c, True).wait_send()
                relay_copy(way, c, False).wait_send()

    @pl.loop(0, heads_kv)
    def _(k):
        out_copy(k).wait()


def solution(mesh):
    n_sec, n_blk, n_tp = mesh.shape["section"], mesh.shape["blk"], mesh.shape["tp"]

    def per_device(query, text_frame, image_feats, image_frame, kv_weight, query_gain, key_gain):
        text = query.shape[0]
        rows, fw = image_feats.shape
        feats, _, kv_cols = kv_weight.shape[1:]
        head = query_gain.shape[1]
        heads_kv = kv_cols // head
        groups = query.shape[1] // kv_cols
        n_chunk = 4
        rc = rows // n_chunk
        w_rows = 1024
        n_stage = 4
        n_group = n_sec // 2 * n_tp
        vmem = pl.BlockSpec(memory_space=pltpu.VMEM)
        dma = pltpu.SemaphoreType.DMA
        if n_sec == 4 and n_blk == 4 and n_tp == 2 and heads_kv == n_chunk:
            anywhere = pl.BlockSpec(memory_space=pl.ANY)
            return pl.pallas_call(
                functools.partial(plane_kernel, (n_sec, n_blk, n_tp, n_chunk)),
                out_shape=jax.ShapeDtypeStruct(query.shape, BF16),
                in_specs=[anywhere, vmem, anywhere, vmem, anywhere, vmem, vmem],
                out_specs=anywhere,
                scratch_shapes=[
                    pltpu.VMEM((feats, 2, kv_cols), BF16),
                    pltpu.VMEM((feats, 2 * kv_cols), BF16),
                    pltpu.VMEM((n_chunk, 2, n_group, rc, fw), BF16),
                    pltpu.VMEM((n_blk, heads_kv, rows, 2 * head), BF16),
                    pltpu.VMEM((n_blk, 1, rows), jnp.int32),
                    pltpu.VMEM(query.shape, BF16),
                    pltpu.VMEM((heads_kv, groups * text, head), BF16),
                    pltpu.VMEM((rc, 2 * kv_cols), F32),
                    pltpu.VMEM((heads_kv, text, groups * head), BF16),
                    dma((feats // fw,)),
                    dma,
                    dma((heads_kv,)),
                    dma((n_chunk,)),
                    dma((n_chunk, 2)),
                    dma((n_chunk, 2)),
                    dma((n_chunk, 2)),
                    dma((n_chunk, 2)),
                    dma((n_chunk, 4)),
                    dma((n_chunk, 4)),
                    dma,
                    dma,
                    dma((2, 4, n_chunk)),
                    dma((2, n_blk, n_chunk)),
                ],
                compiler_params=pltpu.CompilerParams(
                    collective_id=1, has_side_effects=True, vmem_limit_bytes=58 << 20
                ),
            )(
                query,
                text_frame.reshape(1, text),
                image_feats,
                image_frame.reshape(1, rows),
                kv_weight,
                query_gain,
                key_gain,
            )
        return pl.pallas_call(
            functools.partial(kernel, (n_sec, n_blk, n_tp, n_chunk, w_rows)),
            out_shape=jax.ShapeDtypeStruct(query.shape, BF16),
            in_specs=[vmem, vmem, vmem, vmem, pl.BlockSpec(memory_space=pl.ANY), vmem, vmem],
            out_specs=vmem,
            scratch_shapes=[
                pltpu.VMEM((n_stage, w_rows, 2, kv_cols), BF16),
                pltpu.VMEM((feats, 2 * kv_cols), BF16),
                pltpu.VMEM((n_chunk, 2, n_group, rc, fw), BF16),
                pltpu.VMEM((n_blk, n_chunk, rc, 2 * kv_cols), BF16),
                pltpu.VMEM((n_blk, 1, rows), jnp.int32),
                pltpu.VMEM((heads_kv, groups * text, head), BF16),
                pltpu.VMEM((heads_kv, groups * text, head), F32),
                pltpu.VMEM((heads_kv, groups * text, head), F32),
                pltpu.VMEM((rc, 2 * kv_cols), F32),
                dma((n_stage,)),
                dma((n_chunk, 4)),
                dma((n_chunk, 5)),
                dma((n_chunk,)),
                dma((n_chunk,)),
                dma,
                dma,
                dma((2, n_blk, n_chunk)),
                dma((2, n_blk, n_chunk)),
            ],
            compiler_params=pltpu.CompilerParams(
                collective_id=0, has_side_effects=True, vmem_limit_bytes=56 << 20
            ),
        )(
            query,
            text_frame.reshape(1, text),
            image_feats,
            image_frame.reshape(1, rows),
            kv_weight,
            query_gain,
            key_gain,
        )

    return jax.shard_map(
        per_device,
        mesh=mesh,
        in_specs=(
            P(("section", "blk"), "tp"),
            P(("section", "blk")),
            P("blk", ("section", "tp")),
            P("blk"),
            P("section", None, None, "tp"),
            P("section", None),
            P("section", None),
        ),
        out_specs=P(("section", "blk"), "tp"),
        check_vma=False,
    )
```

```python
import functools

import jax
import jax.numpy as jnp
from jax import lax
from jax.experimental import pallas as pl
from jax.experimental.pallas import tpu as pltpu
from jax.sharding import PartitionSpec as P

MESH = pl.DeviceIdType.MESH
BF16 = jnp.bfloat16
F32 = jnp.float32
EPS = 1e-05
PARTS = (2, 2, 2, 2)
EARLY = 3
EXTRA = 2


def kernel(
    dims,
    q_ref, tf_ref, x_ref, fr_ref, w_ref, qg_ref, kg_ref,
    out_ref,
    stage, kvw, xg, kv, frames, qn, acc, tot, proj,
    wsem, fsend, frecv, ssend, srecv, rsend, rrecv, zsend, zrecv,
):
    n_sec, n_blk, n_tp, n_chunk, w_rows = dims
    sec, blk, tp = lax.axis_index("section"), lax.axis_index("blk"), lax.axis_index("tp")
    par = lax.rem(sec, 2)
    half = sec // 2
    mine = half * n_tp + tp
    n_half = n_sec // 2
    n_group = n_half * n_tp
    rows, fw = x_ref.shape
    rc = rows // n_chunk
    feats, _, kv_cols = w_ref.shape[1:]
    head = qg_ref.shape[1]
    heads_kv = kv_cols // head
    text = q_ref.shape[0]
    groups = q_ref.shape[1] // kv_cols
    n_w = feats // w_rows
    n_stage = stage.shape[0]
    sibling = {"section": sec + 1 - 2 * par}

    def w_copy(i):
        return pltpu.make_async_copy(
            w_ref.at[0, pl.ds(i * w_rows, w_rows)], stage.at[i % n_stage], wsem.at[i % n_stage]
        )

    for i in range(min(n_stage, n_w)):
        w_copy(i).start()

    def plane_peer(k):
        other = lax.rem(mine + k, n_group)
        return {"section": 2 * (other // n_tp) + par, "tp": lax.rem(other, n_tp)}

    def line_peer(k):
        return {"blk": lax.rem(blk + k, n_blk)}

    barrier = pltpu.get_barrier_semaphore()
    pl.semaphore_signal(barrier, inc=1, device_id=sibling, device_id_type=MESH)
    for k in range(1, n_group):
        pl.semaphore_signal(barrier, inc=1, device_id=plane_peer(k), device_id_type=MESH)
    for k in range(1, n_blk):
        pl.semaphore_signal(barrier, inc=1, device_id=line_peer(k), device_id_type=MESH)
    pl.semaphore_wait(barrier, n_group + n_blk - 1)

    square = n_half == 2 and n_tp == 2
    near = ({"section": 2 * (1 - half) + par}, {"tp": 1 - tp})
    near_at = ((1 - half) * n_tp + tp, half * n_tp + 1 - tp)

    def feature_copy(c, k):
        return pltpu.make_async_remote_copy(
            src_ref=x_ref.at[pl.ds(c * rc, rc)],
            dst_ref=xg.at[c, par, mine],
            send_sem=fsend.at[c, k if square else 0],
            recv_sem=frecv.at[c, k if square else 2],
            device_id=near[k] if square else plane_peer(k),
            device_id_type=MESH,
        )

    def arrived(c, k):
        return pltpu.make_async_remote_copy(
            src_ref=x_ref.at[pl.ds(c * rc, rc)],
            dst_ref=xg.at[c, par, near_at[k]],
            send_sem=fsend.at[c, k],
            recv_sem=frecv.at[c, k],
            device_id=near[k],
            device_id_type=MESH,
        )

    def corner_copy(c, k, at):
        part = xg.at[c, par, at, pl.ds(k * (rc // 2), rc // 2)]
        return pltpu.make_async_remote_copy(
            src_ref=part,
            dst_ref=part,
            send_sem=fsend.at[c, 2 + k],
            recv_sem=frecv.at[c, 3 + k],
            device_id=near[1 - k],
            device_id_type=MESH,
        )

    def local_copy(c):
        return pltpu.make_async_copy(
            x_ref.at[pl.ds(c * rc, rc)], xg.at[c, par, mine], frecv.at[c, 2]
        )

    def start(c):
        for k in range(2) if square else range(1, n_group):
            feature_copy(c, k).start()
        local_copy(c).start()

    def forward(c):
        if square:
            for k in range(2):
                arrived(c, k).wait_recv()
                corner_copy(c, k, near_at[k]).start()

    start(0)
    if n_chunk > 1:
        start(1)

    def frame_copy(k):
        return pltpu.make_async_remote_copy(
            src_ref=fr_ref,
            dst_ref=frames.at[blk],
            send_sem=rsend,
            recv_sem=rrecv,
            device_id=line_peer(k),
            device_id_type=MESH,
        )

    pltpu.make_async_copy(fr_ref, frames.at[blk], rrecv).start()
    for k in range(1, n_blk):
        frame_copy(k).start()

    def share(c):
        return pltpu.make_async_remote_copy(
            src_ref=xg.at[c, par],
            dst_ref=xg.at[c, par],
            send_sem=ssend.at[c],
            recv_sem=srecv.at[c],
            device_id=sibling,
            device_id_type=MESH,
        )

    def pass_on(c):
        if square:
            local_copy(c).wait()
            for k in range(2):
                corner_copy(c, k, (1 - half) * n_tp + 1 - tp).wait_recv()
        else:
            pltpu.make_async_copy(xg.at[c, par], xg.at[c, par], frecv.at[c, 2]).wait()
        share(c).start()

    sub = 2 * head
    ri = lax.broadcasted_iota(jnp.int32, (sub, sub), 0)
    ci = lax.broadcasted_iota(jnp.int32, (sub, sub), 1)
    take = (ci == 2 * lax.rem(ri, head) + ri // head).astype(BF16)
    for i in range(n_w):
        w_copy(i).wait()

        @pl.loop(0, w_rows // head, unroll=4)
        def _(j):
            at = pl.multiple_of(j * head, head)
            block = stage[i % n_stage, pl.ds(at, head)].reshape(sub, kv_cols)
            apart = jnp.dot(take, block, preferred_element_type=F32).astype(BF16)
            to = pl.multiple_of(i * w_rows + j * head, head)
            kvw[pl.ds(to, head), :kv_cols] = apart[:head]
            kvw[pl.ds(to, head), kv_cols:] = apart[head:]

        if i + n_stage < n_w:
            w_copy(i + n_stage).start()
        if i == n_w // 8:
            forward(0)
            if n_chunk > 2:
                start(2)
        if i == (3 * n_w) // 8:
            pass_on(0)
        if i == (5 * n_w) // 8 and n_chunk > 1:
            forward(1)
            if n_chunk > 3:
                start(3)

    def line_copy(way, src, d, c):
        to = blk + 1 if way == 0 else blk - 1
        return pltpu.make_async_remote_copy(
            src_ref=kv.at[src, c],
            dst_ref=kv.at[src, c],
            send_sem=zsend.at[way, d - 1, c],
            recv_sem=zrecv.at[way, d - 1, c],
            device_id={"blk": to},
            device_id_type=MESH,
        )

    can = (blk + 1 < n_blk, blk >= 1)

    def source(way, d):
        return blk - d if way == 0 else blk + d

    def exists(way, d):
        return blk - d >= 0 if way == 0 else blk + d < n_blk

    def relay(way, d, c):
        @pl.when(exists(way, d))
        def _():
            src = source(way, d)
            line_copy(way, src, d, c).wait_recv()

            @pl.when(can[way])
            def _():
                line_copy(way, src, d + 1, c).start()

    for c in range(n_chunk):
        share(c).wait_recv()
        proj[...] = jnp.zeros_like(proj)

        @pl.loop(0, n_group, unroll=2)
        def _(j):
            for p in range(2):
                place = ((2 * (j // n_tp) + p) * n_tp + lax.rem(j, n_tp)) * fw
                part = kvw[pl.ds(pl.multiple_of(place, fw), fw), :]
                proj[...] += jnp.dot(xg[c, p, j], part, preferred_element_type=F32)

        for h in range(heads_kv):
            key = proj[:, h * head:(h + 1) * head]
            scale = lax.rsqrt(jnp.mean(key * key, axis=-1, keepdims=True) + EPS)
            kv[blk, c, :, h * head:(h + 1) * head] = (key * scale * kg_ref[...]).astype(BF16)
        kv[blk, c, :, kv_cols:] = proj[:, kv_cols:].astype(BF16)
        for way in range(2):
            @pl.when(can[way])
            def _():
                line_copy(way, blk, 1, c).start()
        if c + 1 < n_chunk:
            pass_on(c + 1)
        if c >= 1:
            for way in range(2):
                relay(way, 1, c - 1)
        if c + 2 < n_chunk:
            forward(c + 2)
        if c + 4 < n_chunk:
            start(c + 4)

    gain = qg_ref[...] * head ** (-0.5)

    @pl.loop(0, heads_kv)
    def _(k):
        for g in range(groups):
            col = pl.multiple_of((k * groups + g) * head, head)
            rowsq = q_ref[:, pl.ds(col, head)].astype(F32)
            scale = lax.rsqrt(jnp.mean(rowsq * rowsq, axis=-1, keepdims=True) + EPS)
            qn[k, g * text:(g + 1) * text, :] = (rowsq * scale * gain).astype(BF16)

    pltpu.make_async_copy(frames, frames, rrecv).wait()
    limit = jnp.broadcast_to(tf_ref[...], (text, text)).T[:, :1]
    acc[...] = jnp.zeros_like(acc)
    tot[...] = jnp.zeros_like(tot)

    def attend(src):
        allowed = frames[src] <= limit

        @pl.loop(0, heads_kv)
        def _(k):
            at = pl.multiple_of(k * head, head)
            keys = kv[src, :, :, pl.ds(at, head)].reshape(rows, head)
            values = kv[src, :, :, pl.ds(kv_cols + at, head)].reshape(rows, head)
            for g in range(groups):
                span = slice(g * text, (g + 1) * text)
                scores = lax.dot_general(
                    qn[k, span, :], keys, (((1,), (1,)), ((), ())), preferred_element_type=F32
                )
                weights = jnp.where(allowed, jnp.exp(scores), 0.0)
                total = weights[:, :head]
                for m in range(1, rows // head):
                    total = total + weights[:, m * head:(m + 1) * head]
                tot[k, span, :] += total
                acc[k, span, :] += jnp.dot(
                    weights.astype(BF16), values, preferred_element_type=F32
                )

    def attend_if(way, d):
        @pl.when(exists(way, d))
        def _():
            attend(source(way, d))

    for way in range(2):
        relay(way, 1, n_chunk - 1)
    attend(blk)

    @pl.loop(1, n_blk - 1)
    def _(d):
        for c in range(n_chunk):
            for way in range(2):
                relay(way, d + 1, c)
            if c < 2:
                attend_if(c, d)

    for way in range(2):
        attend_if(way, n_blk - 1)

    @pl.loop(0, heads_kv)
    def _(k):
        for g in range(groups):
            span = slice(g * text, (g + 1) * text)
            total = jnp.sum(tot[k, span, :], axis=-1, keepdims=True)
            col = pl.multiple_of((k * groups + g) * head, head)
            out_ref[:, pl.ds(col, head)] = (acc[k, span, :] / total).astype(BF16)

    for c in range(n_chunk):
        if square:
            for k in range(2):
                feature_copy(c, k).wait_send()
                corner_copy(c, k, near_at[k]).wait_send()
        elif n_group > 1:
            gone = xg.at[c, par, pl.ds(0, n_group - 1)]
            pltpu.make_async_copy(gone, gone, fsend.at[c, 0]).wait()
        share(c).wait_send()
    if n_blk > 1:
        gone = frames.at[pl.ds(0, n_blk - 1)]
        pltpu.make_async_copy(gone, gone, rsend).wait()

    @pl.loop(1, n_blk)
    def _(d):
        for way in range(2):
            @pl.when(can[way] & exists(way, d - 1))
            def _():
                for c in range(n_chunk):
                    line_copy(way, source(way, d - 1), d, c).wait_send()


def plane_kernel(
    dims,
    q_ref, tf_ref, x_ref, fr_ref, w_ref, qg_ref, kg_ref,
    out_ref,
    raw, kvw, xg, kv, frames, qv, qn, proj, outv,
    wsem, qsem, osem, lsem, nsend, nrecv, csend, crecv, ssend, srecv, xsend, xrecv,
    rsend, rrecv, zsend, zrecv, hsend, hrecv, ready,
):
    n_sec, n_blk, n_tp, sizes, n_early, n_extra = dims
    n_chunk = len(sizes)
    sizes = sizes + sizes[n_chunk - n_extra:]
    n_all = n_chunk + n_extra
    first = [sum(sizes[:c]) for c in range(n_all)]
    sec, blk, tp = lax.axis_index("section"), lax.axis_index("blk"), lax.axis_index("tp")
    par = lax.rem(sec, 2)
    half = sec // 2
    rows, fw = x_ref.shape
    feats, _, kv_cols = w_ref.shape[1:]
    head = qg_ref.shape[1]
    heads_kv = kv_cols // head
    text = qv.shape[0]
    groups = qv.shape[1] // kv_cols
    n_slice = feats // fw
    last = n_blk - 1

    mine = half * n_tp + tp
    other = 2 * (1 - half) + par
    near = ({"section": other}, {"tp": 1 - tp})
    slots = (
        mine,
        (1 - half) * n_tp + tp,
        half * n_tp + 1 - tp,
        (1 - half) * n_tp + 1 - tp,
    )
    sibling = {"section": sec + 1 - 2 * par}

    x_copy = pltpu.make_async_copy(x_ref, xg.at[par, mine, pl.ds(0, rows)], lsem)

    def w_copy(i):
        span = pl.ds(i * fw, fw)
        return pltpu.make_async_copy(w_ref.at[0, span], raw.at[span], wsem.at[i])

    q_copy = pltpu.make_async_copy(q_ref, qv, qsem)
    x_copy.start()
    for i in range(n_slice):
        w_copy(i).start()
    q_copy.start()

    def line_peer(k):
        return {"blk": lax.rem(blk + k, n_blk)}

    def along(way):
        return blk if way == 0 else last - blk

    def at(way, u):
        return u if way == 0 else last - u

    barrier = pltpu.get_barrier_semaphore()
    for peer in (sibling, *near):
        pl.semaphore_signal(barrier, inc=1, device_id=peer, device_id_type=MESH)
    for way in range(2):
        @pl.when(along(way) < last)
        def _():
            ahead = {"blk": at(way, along(way) + 1)}
            pl.semaphore_signal(barrier, inc=1, device_id=ahead, device_id_type=MESH)

    inner = (blk > 0) & (blk < last)
    pl.semaphore_wait(barrier, 4 + inner.astype(jnp.int32))

    def tell(way, hops):
        ahead = {"blk": at(way, along(way) + 1)}
        pl.semaphore_signal(ready.at[way, hops], inc=1, device_id=ahead, device_id_type=MESH)

    def hear_far():
        for way in range(2):
            @pl.when(along(way) >= 2)
            def _():
                pl.semaphore_wait(ready.at[way, 0], 1)

            @pl.when(along(way) == 2)
            def _():
                tell(way, 1)

            @pl.when(along(way) == last)
            def _():
                pl.semaphore_wait(ready.at[way, 1], 1)

    def near_copy(c, k, slot):
        part = xg.at[par, slot, pl.ds(first[c], sizes[c])]
        return pltpu.make_async_remote_copy(
            src_ref=part,
            dst_ref=part,
            send_sem=nsend.at[c, k],
            recv_sem=nrecv.at[c, k],
            device_id=near[k],
            device_id_type=MESH,
        )

    def corner_copy(c, k, slot):
        part = xg.at[par, slot, pl.ds(first[c] + k * (sizes[c] // 2), sizes[c] // 2)]
        return pltpu.make_async_remote_copy(
            src_ref=part,
            dst_ref=part,
            send_sem=csend.at[c, k],
            recv_sem=crecv.at[c, k],
            device_id=near[1 - k],
            device_id_type=MESH,
        )

    def share(c, i, side):
        start, size = first[c], sizes[c]
        if i == 0 and c == 0:
            start, size = 0, rows
        part = xg.at[side, slots[i], pl.ds(start, size)]
        return pltpu.make_async_remote_copy(
            src_ref=part,
            dst_ref=part,
            send_sem=ssend.at[c, i],
            recv_sem=srecv.at[c, i],
            device_id=sibling,
            device_id_type=MESH,
        )

    def start(c):
        for k in range(2):
            near_copy(c, k, mine).start()
        if c == 0 or c >= n_chunk:
            share(c, 0, par).start()

    def forward(c):
        for k in range(2):
            near_copy(c, k, slots[k + 1]).wait_recv()
            corner_copy(c, k, slots[k + 1]).start()
            share(c, k + 1, par).start()

    def turn(c):
        for k in range(2):
            corner_copy(c, k, slots[3]).wait_recv()
        share(c, 3, par).start()

    at_end = (blk == 0) | (blk == last)

    def extra_copy(way, e):
        c = n_chunk - n_extra + e
        return pltpu.make_async_remote_copy(
            src_ref=xg.at[par, mine, pl.ds(first[c], sizes[c])],
            dst_ref=xg.at[par, mine, pl.ds(first[n_chunk + e], sizes[c])],
            send_sem=xsend.at[e],
            recv_sem=xrecv.at[e],
            device_id={"blk": at(way, last)},
            device_id_type=MESH,
        )

    def start_extra():
        if n_extra > 0:
            @pl.when(at_end)
            def _():
                for e in range(n_extra):
                    extra_copy(0, e).wait_recv()
                    start(n_chunk + e)

    def frame_copy(k):
        return pltpu.make_async_remote_copy(
            src_ref=fr_ref,
            dst_ref=frames.at[blk],
            send_sem=rsend,
            recv_sem=rrecv,
            device_id=line_peer(k),
            device_id_type=MESH,
        )

    x_copy.wait()
    start(0)
    start(1)
    for way in range(2):
        @pl.when(along(way) == 2)
        def _():
            for e in range(n_extra):
                extra_copy(way, e).start()

    for way in range(2):
        @pl.when((along(way) >= 1) & (along(way) < last))
        def _():
            tell(way, 0)

    pltpu.make_async_copy(fr_ref, frames.at[blk], rrecv).start()

    part = fw // 2
    for i in range(n_slice):
        w_copy(i).wait()

        @pl.loop(0, fw // part, unroll=2)
        def _(j):
            span = pl.ds(pl.multiple_of(i * fw + j * part, part), part)
            kvw[span, :] = raw[span].reshape(part, 2 * kv_cols)

        if i == n_slice - 1:
            forward(0)
            start(2)

    hear_far()
    for k in range(1, n_blk):
        frame_copy(k).start()

    def line_copy(way, kind, src, to, c):
        piece = kv.at[src, :, pl.ds(first[c], sizes[c])]
        return pltpu.make_async_remote_copy(
            src_ref=piece,
            dst_ref=piece,
            send_sem=zsend.at[way, kind, c],
            recv_sem=zrecv.at[way, src, c],
            device_id={"blk": to},
            device_id_type=MESH,
        )

    def hop(way, c):
        return line_copy(way, 0, blk, at(way, along(way) + 1), c)

    def hops(way, c):
        return along(way) < (last if c < n_chunk - n_extra else 2)

    def relay_copy(way, d, c):
        u = along(way)
        return line_copy(way, d, at(way, u - d), at(way, u + 1), c)

    def head_copy(way, h):
        piece = kv.at[at(way, 0), h, pl.ds(first[n_early], rows - first[n_early])]
        return pltpu.make_async_remote_copy(
            src_ref=piece,
            dst_ref=piece,
            send_sem=hsend.at[way, h],
            recv_sem=hrecv.at[way, h],
            device_id={"blk": at(way, last)},
            device_id_type=MESH,
        )

    def arrived(way, u, c):
        line_copy(way, 0, at(way, u), blk, c).wait_recv()

    def send(c):
        for way in range(2):
            @pl.when(hops(way, c))
            def _():
                hop(way, c).start()

    def passes(way, d):
        return (along(way) >= d) & (along(way) < last)

    def relay(d, c):
        if d < 2 or c < n_early:
            for way in range(2):
                @pl.when(passes(way, d))
                def _():
                    arrived(way, along(way) - d, c)
                    relay_copy(way, d, c).start()

    def weight(p, slot):
        place = ((2 * (slot // n_tp) + p) * n_tp + lax.rem(slot, n_tp)) * fw
        return kvw[pl.ds(pl.multiple_of(place, fw), fw), :]

    proj[:rows, :] = jnp.dot(xg[par, mine, :rows, :], weight(par, mine), preferred_element_type=F32)
    share(0, 0, 1 - par).wait_recv()
    proj[:rows, :] += jnp.dot(xg[1 - par, mine, :rows, :], weight(1 - par, mine), preferred_element_type=F32)

    def add(c, i):
        span = slice(first[c], first[c] + sizes[c])
        for p in range(2):
            proj[span, :] += jnp.dot(
                xg[p, slots[i], span, :], weight(p, slots[i]), preferred_element_type=F32
            )

    def add_near(c):
        for i in (1, 2):
            share(c, i, 1 - par).wait_recv()
            add(c, i)

    def add_corner(c):
        share(c, 3, 1 - par).wait_recv()
        add(c, 3)

    def finish(c, src, to):
        span = slice(first[c], first[c] + sizes[c])
        for h in range(heads_kv):
            key = proj[span, h * head:(h + 1) * head]
            scale = lax.rsqrt(jnp.mean(key * key, axis=-1, keepdims=True) + EPS)
            kv[src, h, to:to + sizes[c], :head] = (key * scale * kg_ref[...]).astype(BF16)
            kv[src, h, to:to + sizes[c], head:] = (
                proj[span, kv_cols + h * head:kv_cols + (h + 1) * head].astype(BF16)
            )

    for c in range(n_chunk):
        add_near(c)
        if c + 1 < n_chunk:
            forward(c + 1)
            if c + 3 < n_chunk:
                start(c + 3)
            if c + 2 == n_chunk:
                start_extra()
        if c >= 2:
            relay(1, c - 2)
        if c >= 3:
            relay(2, c - 3)
        turn(c)
        add_corner(c)
        finish(c, blk, first[c])
        send(c)

    relay(1, n_chunk - 2)
    relay(2, n_chunk - 3)
    relay(1, n_chunk - 1)
    for c in range(n_chunk - 2, n_chunk):
        relay(2, c)

    for way in range(2):
        @pl.when(along(way) == 2)
        def _():
            for c in range(n_early, n_chunk):
                arrived(way, 0, c)
            for h in range(heads_kv):
                head_copy(way, h).start()

    if n_extra > 0:
        @pl.when(at_end)
        def _():
            beside = jnp.where(blk == 0, 1, last - 1)
            for c in range(n_chunk, n_all):
                span = slice(first[c], first[c] + sizes[c])
                proj[span, :] = jnp.zeros((sizes[c], proj.shape[1]), F32)
                share(c, 0, 1 - par).wait_recv()
                add(c, 0)
                forward(c)
                add_near(c)
                turn(c)
                add_corner(c)
                finish(c, beside, first[c - n_extra])

    q_copy.wait()
    gain = qg_ref[...] * head ** (-0.5)

    @pl.loop(0, heads_kv)
    def _(k):
        for g in range(groups):
            col = pl.multiple_of((k * groups + g) * head, head)
            rowsq = qv[:, pl.ds(col, head)].astype(F32)
            scale = lax.rsqrt(jnp.mean(rowsq * rowsq, axis=-1, keepdims=True) + EPS)
            qn[k, g * text:(g + 1) * text, :] = (rowsq * scale * gain).astype(BF16)

    pltpu.make_async_copy(frames, frames, rrecv).wait()
    limit = jnp.broadcast_to(tf_ref[...], (text, text)).T[:, :1]
    allowed = jnp.concatenate([frames[s] for s in range(n_blk)], axis=1) <= limit

    for way in range(2):
        @pl.when(along(way) == last)
        def _():
            for c in range(n_chunk - n_extra):
                arrived(way, 2, c)
            for c in range(n_chunk):
                arrived(way, 1, c)
            for c in range(n_early):
                arrived(way, 0, c)

    def out_copy(k):
        return pltpu.make_async_copy(
            outv.at[k], out_ref.at[:, pl.ds(pl.multiple_of(k * groups * head, head), groups * head)], osem.at[k]
        )

    @pl.loop(0, heads_kv)
    def _(k):
        for way in range(2):
            @pl.when(along(way) == last)
            def _():
                head_copy(way, k).wait_recv()

        keys = jnp.concatenate([kv[s, k, :, :head] for s in range(n_blk)], axis=0)
        values = jnp.concatenate([kv[s, k, :, head:] for s in range(n_blk)], axis=0)
        n_rows = groups * text
        scores = lax.dot_general(
            qn[k], keys, (((1,), (1,)), ((), ())), preferred_element_type=F32
        )
        weights = jnp.where(
            allowed[None], jnp.exp(scores).reshape(groups, text, n_blk * rows), 0.0
        ).reshape(n_rows, n_blk * rows)
        total = weights[:, :head]
        for m in range(1, n_blk * rows // head):
            total = total + weights[:, m * head:(m + 1) * head]
        total = jnp.sum(total, axis=-1, keepdims=True)
        result = jnp.dot(weights.astype(BF16), values, preferred_element_type=F32)
        result = (result / total).astype(BF16)
        for g in range(groups):
            outv[k, :, g * head:(g + 1) * head] = result[g * text:(g + 1) * text]
        out_copy(k).start()

    def sent(c):
        for k in range(2):
            near_copy(c, k, mine).wait_send()
            corner_copy(c, k, slots[k + 1]).wait_send()
        for i in range(4):
            if i > 0 or c == 0 or c >= n_chunk:
                share(c, i, par).wait_send()

    for c in range(n_chunk):
        sent(c)
    if n_extra > 0:
        @pl.when(at_end)
        def _():
            for c in range(n_chunk, n_all):
                sent(c)

        @pl.when(jnp.logical_not(at_end))
        def _():
            for e in range(n_extra):
                extra_copy(0, e).wait_send()

    gone = frames.at[pl.ds(0, n_blk - 1)]
    pltpu.make_async_copy(gone, gone, rsend).wait()
    for way in range(2):
        for c in range(n_chunk):
            @pl.when(hops(way, c))
            def _():
                hop(way, c).wait_send()

            @pl.when(passes(way, 1))
            def _():
                relay_copy(way, 1, c).wait_send()

            if c < n_early:
                @pl.when(passes(way, 2))
                def _():
                    relay_copy(way, 2, c).wait_send()

        @pl.when(along(way) == 2)
        def _():
            for h in range(heads_kv):
                head_copy(way, h).wait_send()

    @pl.loop(0, heads_kv)
    def _(k):
        out_copy(k).wait()


def solution(mesh):
    n_sec, n_blk, n_tp = mesh.shape["section"], mesh.shape["blk"], mesh.shape["tp"]

    def per_device(query, text_frame, image_feats, image_frame, kv_weight, query_gain, key_gain):
        text = query.shape[0]
        rows, fw = image_feats.shape
        feats, _, kv_cols = kv_weight.shape[1:]
        head = query_gain.shape[1]
        heads_kv = kv_cols // head
        groups = query.shape[1] // kv_cols
        n_chunk = 4
        rc = rows // n_chunk
        w_rows = 1024
        n_stage = 4
        n_group = n_sec // 2 * n_tp
        vmem = pl.BlockSpec(memory_space=pltpu.VMEM)
        dma = pltpu.SemaphoreType.DMA
        if n_sec == 4 and n_blk == 4 and n_tp == 2 and rows % 128 == 0:
            sizes = tuple(rows * part // 8 for part in PARTS)
            n_part = len(sizes)
            n_all = n_part + EXTRA
            taller = rows + sum(sizes[n_part - EXTRA:])
            anywhere = pl.BlockSpec(memory_space=pl.ANY)
            return pl.pallas_call(
                functools.partial(plane_kernel, (n_sec, n_blk, n_tp, sizes, EARLY, EXTRA)),
                out_shape=jax.ShapeDtypeStruct(query.shape, BF16),
                in_specs=[anywhere, vmem, anywhere, vmem, anywhere, vmem, vmem],
                out_specs=anywhere,
                scratch_shapes=[
                    pltpu.VMEM((feats, 2, kv_cols), BF16),
                    pltpu.VMEM((feats, 2 * kv_cols), BF16),
                    pltpu.VMEM((2, n_group, taller, fw), BF16),
                    pltpu.VMEM((n_blk, heads_kv, rows, 2 * head), BF16),
                    pltpu.VMEM((n_blk, 1, rows), jnp.int32),
                    pltpu.VMEM(query.shape, BF16),
                    pltpu.VMEM((heads_kv, groups * text, head), BF16),
                    pltpu.VMEM((taller, 2 * kv_cols), F32),
                    pltpu.VMEM((heads_kv, text, groups * head), BF16),
                    dma((feats // fw,)),
                    dma,
                    dma((heads_kv,)),
                    dma,
                    dma((n_all, 2)),
                    dma((n_all, 2)),
                    dma((n_all, 2)),
                    dma((n_all, 2)),
                    dma((n_all, 4)),
                    dma((n_all, 4)),
                    dma((max(EXTRA, 1),)),
                    dma((max(EXTRA, 1),)),
                    dma,
                    dma,
                    dma((2, 4, n_part)),
                    dma((2, n_blk, n_part)),
                    dma((2, heads_kv)),
                    dma((2, heads_kv)),
                    pltpu.SemaphoreType.REGULAR((2, 2)),
                ],
                compiler_params=pltpu.CompilerParams(
                    collective_id=1, has_side_effects=True, vmem_limit_bytes=58 << 20
                ),
            )(
                query,
                text_frame.reshape(1, text),
                image_feats,
                image_frame.reshape(1, rows),
                kv_weight,
                query_gain,
                key_gain,
            )
        return pl.pallas_call(
            functools.partial(kernel, (n_sec, n_blk, n_tp, n_chunk, w_rows)),
            out_shape=jax.ShapeDtypeStruct(query.shape, BF16),
            in_specs=[vmem, vmem, vmem, vmem, pl.BlockSpec(memory_space=pl.ANY), vmem, vmem],
            out_specs=vmem,
            scratch_shapes=[
                pltpu.VMEM((n_stage, w_rows, 2, kv_cols), BF16),
                pltpu.VMEM((feats, 2 * kv_cols), BF16),
                pltpu.VMEM((n_chunk, 2, n_group, rc, fw), BF16),
                pltpu.VMEM((n_blk, n_chunk, rc, 2 * kv_cols), BF16),
                pltpu.VMEM((n_blk, 1, rows), jnp.int32),
                pltpu.VMEM((heads_kv, groups * text, head), BF16),
                pltpu.VMEM((heads_kv, groups * text, head), F32),
                pltpu.VMEM((heads_kv, groups * text, head), F32),
                pltpu.VMEM((rc, 2 * kv_cols), F32),
                dma((n_stage,)),
                dma((n_chunk, 4)),
                dma((n_chunk, 5)),
                dma((n_chunk,)),
                dma((n_chunk,)),
                dma,
                dma,
                dma((2, n_blk, n_chunk)),
                dma((2, n_blk, n_chunk)),
            ],
            compiler_params=pltpu.CompilerParams(
                collective_id=0, has_side_effects=True, vmem_limit_bytes=56 << 20
            ),
        )(
            query,
            text_frame.reshape(1, text),
            image_feats,
            image_frame.reshape(1, rows),
            kv_weight,
            query_gain,
            key_gain,
        )

    return jax.shard_map(
        per_device,
        mesh=mesh,
        in_specs=(
            P(("section", "blk"), "tp"),
            P(("section", "blk")),
            P("blk", ("section", "tp")),
            P("blk"),
            P("section", None, None, "tp"),
            P("section", None),
            P("section", None),
        ),
        out_specs=P(("section", "blk"), "tp"),
        check_vma=False,
    )
```

```python
import functools

import jax
import jax.numpy as jnp
from jax import lax
from jax.experimental import pallas as pl
from jax.experimental.pallas import tpu as pltpu
from jax.sharding import PartitionSpec as P

MESH = pl.DeviceIdType.MESH
BF16 = jnp.bfloat16
F32 = jnp.float32
EPS = 1e-05
PARTS = (2, 2, 2, 2)
EARLY = 3
EXTRA = 2


def kernel(
    dims,
    q_ref, tf_ref, x_ref, fr_ref, w_ref, qg_ref, kg_ref,
    out_ref,
    stage, kvw, xg, kv, frames, qn, acc, tot, proj,
    wsem, fsend, frecv, ssend, srecv, rsend, rrecv, zsend, zrecv,
):
    n_sec, n_blk, n_tp, n_chunk, w_rows = dims
    sec, blk, tp = lax.axis_index("section"), lax.axis_index("blk"), lax.axis_index("tp")
    par = lax.rem(sec, 2)
    half = sec // 2
    mine = half * n_tp + tp
    n_half = n_sec // 2
    n_group = n_half * n_tp
    rows, fw = x_ref.shape
    rc = rows // n_chunk
    feats, _, kv_cols = w_ref.shape[1:]
    head = qg_ref.shape[1]
    heads_kv = kv_cols // head
    text = q_ref.shape[0]
    groups = q_ref.shape[1] // kv_cols
    n_w = feats // w_rows
    n_stage = stage.shape[0]
    sibling = {"section": sec + 1 - 2 * par}

    def w_copy(i):
        return pltpu.make_async_copy(
            w_ref.at[0, pl.ds(i * w_rows, w_rows)], stage.at[i % n_stage], wsem.at[i % n_stage]
        )

    for i in range(min(n_stage, n_w)):
        w_copy(i).start()

    def plane_peer(k):
        other = lax.rem(mine + k, n_group)
        return {"section": 2 * (other // n_tp) + par, "tp": lax.rem(other, n_tp)}

    def line_peer(k):
        return {"blk": lax.rem(blk + k, n_blk)}

    barrier = pltpu.get_barrier_semaphore()
    pl.semaphore_signal(barrier, inc=1, device_id=sibling, device_id_type=MESH)
    for k in range(1, n_group):
        pl.semaphore_signal(barrier, inc=1, device_id=plane_peer(k), device_id_type=MESH)
    for k in range(1, n_blk):
        pl.semaphore_signal(barrier, inc=1, device_id=line_peer(k), device_id_type=MESH)
    pl.semaphore_wait(barrier, n_group + n_blk - 1)

    square = n_half == 2 and n_tp == 2
    near = ({"section": 2 * (1 - half) + par}, {"tp": 1 - tp})
    near_at = ((1 - half) * n_tp + tp, half * n_tp + 1 - tp)

    def feature_copy(c, k):
        return pltpu.make_async_remote_copy(
            src_ref=x_ref.at[pl.ds(c * rc, rc)],
            dst_ref=xg.at[c, par, mine],
            send_sem=fsend.at[c, k if square else 0],
            recv_sem=frecv.at[c, k if square else 2],
            device_id=near[k] if square else plane_peer(k),
            device_id_type=MESH,
        )

    def arrived(c, k):
        return pltpu.make_async_remote_copy(
            src_ref=x_ref.at[pl.ds(c * rc, rc)],
            dst_ref=xg.at[c, par, near_at[k]],
            send_sem=fsend.at[c, k],
            recv_sem=frecv.at[c, k],
            device_id=near[k],
            device_id_type=MESH,
        )

    def corner_copy(c, k, at):
        part = xg.at[c, par, at, pl.ds(k * (rc // 2), rc // 2)]
        return pltpu.make_async_remote_copy(
            src_ref=part,
            dst_ref=part,
            send_sem=fsend.at[c, 2 + k],
            recv_sem=frecv.at[c, 3 + k],
            device_id=near[1 - k],
            device_id_type=MESH,
        )

    def local_copy(c):
        return pltpu.make_async_copy(
            x_ref.at[pl.ds(c * rc, rc)], xg.at[c, par, mine], frecv.at[c, 2]
        )

    def start(c):
        for k in range(2) if square else range(1, n_group):
            feature_copy(c, k).start()
        local_copy(c).start()

    def forward(c):
        if square:
            for k in range(2):
                arrived(c, k).wait_recv()
                corner_copy(c, k, near_at[k]).start()

    start(0)
    if n_chunk > 1:
        start(1)

    def frame_copy(k):
        return pltpu.make_async_remote_copy(
            src_ref=fr_ref,
            dst_ref=frames.at[blk],
            send_sem=rsend,
            recv_sem=rrecv,
            device_id=line_peer(k),
            device_id_type=MESH,
        )

    pltpu.make_async_copy(fr_ref, frames.at[blk], rrecv).start()
    for k in range(1, n_blk):
        frame_copy(k).start()

    def share(c):
        return pltpu.make_async_remote_copy(
            src_ref=xg.at[c, par],
            dst_ref=xg.at[c, par],
            send_sem=ssend.at[c],
            recv_sem=srecv.at[c],
            device_id=sibling,
            device_id_type=MESH,
        )

    def pass_on(c):
        if square:
            local_copy(c).wait()
            for k in range(2):
                corner_copy(c, k, (1 - half) * n_tp + 1 - tp).wait_recv()
        else:
            pltpu.make_async_copy(xg.at[c, par], xg.at[c, par], frecv.at[c, 2]).wait()
        share(c).start()

    sub = 2 * head
    ri = lax.broadcasted_iota(jnp.int32, (sub, sub), 0)
    ci = lax.broadcasted_iota(jnp.int32, (sub, sub), 1)
    take = (ci == 2 * lax.rem(ri, head) + ri // head).astype(BF16)
    for i in range(n_w):
        w_copy(i).wait()

        @pl.loop(0, w_rows // head, unroll=4)
        def _(j):
            at = pl.multiple_of(j * head, head)
            block = stage[i % n_stage, pl.ds(at, head)].reshape(sub, kv_cols)
            apart = jnp.dot(take, block, preferred_element_type=F32).astype(BF16)
            to = pl.multiple_of(i * w_rows + j * head, head)
            kvw[pl.ds(to, head), :kv_cols] = apart[:head]
            kvw[pl.ds(to, head), kv_cols:] = apart[head:]

        if i + n_stage < n_w:
            w_copy(i + n_stage).start()
        if i == n_w // 8:
            forward(0)
            if n_chunk > 2:
                start(2)
        if i == (3 * n_w) // 8:
            pass_on(0)
        if i == (5 * n_w) // 8 and n_chunk > 1:
            forward(1)
            if n_chunk > 3:
                start(3)

    def line_copy(way, src, d, c):
        to = blk + 1 if way == 0 else blk - 1
        return pltpu.make_async_remote_copy(
            src_ref=kv.at[src, c],
            dst_ref=kv.at[src, c],
            send_sem=zsend.at[way, d - 1, c],
            recv_sem=zrecv.at[way, d - 1, c],
            device_id={"blk": to},
            device_id_type=MESH,
        )

    can = (blk + 1 < n_blk, blk >= 1)

    def source(way, d):
        return blk - d if way == 0 else blk + d

    def exists(way, d):
        return blk - d >= 0 if way == 0 else blk + d < n_blk

    def relay(way, d, c):
        @pl.when(exists(way, d))
        def _():
            src = source(way, d)
            line_copy(way, src, d, c).wait_recv()

            @pl.when(can[way])
            def _():
                line_copy(way, src, d + 1, c).start()

    for c in range(n_chunk):
        share(c).wait_recv()
        proj[...] = jnp.zeros_like(proj)

        @pl.loop(0, n_group, unroll=2)
        def _(j):
            for p in range(2):
                place = ((2 * (j // n_tp) + p) * n_tp + lax.rem(j, n_tp)) * fw
                part = kvw[pl.ds(pl.multiple_of(place, fw), fw), :]
                proj[...] += jnp.dot(xg[c, p, j], part, preferred_element_type=F32)

        for h in range(heads_kv):
            key = proj[:, h * head:(h + 1) * head]
            scale = lax.rsqrt(jnp.mean(key * key, axis=-1, keepdims=True) + EPS)
            kv[blk, c, :, h * head:(h + 1) * head] = (key * scale * kg_ref[...]).astype(BF16)
        kv[blk, c, :, kv_cols:] = proj[:, kv_cols:].astype(BF16)
        for way in range(2):
            @pl.when(can[way])
            def _():
                line_copy(way, blk, 1, c).start()
        if c + 1 < n_chunk:
            pass_on(c + 1)
        if c >= 1:
            for way in range(2):
                relay(way, 1, c - 1)
        if c + 2 < n_chunk:
            forward(c + 2)
        if c + 4 < n_chunk:
            start(c + 4)

    gain = qg_ref[...] * head ** (-0.5)

    @pl.loop(0, heads_kv)
    def _(k):
        for g in range(groups):
            col = pl.multiple_of((k * groups + g) * head, head)
            rowsq = q_ref[:, pl.ds(col, head)].astype(F32)
            scale = lax.rsqrt(jnp.mean(rowsq * rowsq, axis=-1, keepdims=True) + EPS)
            qn[k, g * text:(g + 1) * text, :] = (rowsq * scale * gain).astype(BF16)

    pltpu.make_async_copy(frames, frames, rrecv).wait()
    limit = jnp.broadcast_to(tf_ref[...], (text, text)).T[:, :1]
    acc[...] = jnp.zeros_like(acc)
    tot[...] = jnp.zeros_like(tot)

    def attend(src):
        allowed = frames[src] <= limit

        @pl.loop(0, heads_kv)
        def _(k):
            at = pl.multiple_of(k * head, head)
            keys = kv[src, :, :, pl.ds(at, head)].reshape(rows, head)
            values = kv[src, :, :, pl.ds(kv_cols + at, head)].reshape(rows, head)
            for g in range(groups):
                span = slice(g * text, (g + 1) * text)
                scores = lax.dot_general(
                    qn[k, span, :], keys, (((1,), (1,)), ((), ())), preferred_element_type=F32
                )
                weights = jnp.where(allowed, jnp.exp(scores), 0.0)
                total = weights[:, :head]
                for m in range(1, rows // head):
                    total = total + weights[:, m * head:(m + 1) * head]
                tot[k, span, :] += total
                acc[k, span, :] += jnp.dot(
                    weights.astype(BF16), values, preferred_element_type=F32
                )

    def attend_if(way, d):
        @pl.when(exists(way, d))
        def _():
            attend(source(way, d))

    for way in range(2):
        relay(way, 1, n_chunk - 1)
    attend(blk)

    @pl.loop(1, n_blk - 1)
    def _(d):
        for c in range(n_chunk):
            for way in range(2):
                relay(way, d + 1, c)
            if c < 2:
                attend_if(c, d)

    for way in range(2):
        attend_if(way, n_blk - 1)

    @pl.loop(0, heads_kv)
    def _(k):
        for g in range(groups):
            span = slice(g * text, (g + 1) * text)
            total = jnp.sum(tot[k, span, :], axis=-1, keepdims=True)
            col = pl.multiple_of((k * groups + g) * head, head)
            out_ref[:, pl.ds(col, head)] = (acc[k, span, :] / total).astype(BF16)

    for c in range(n_chunk):
        if square:
            for k in range(2):
                feature_copy(c, k).wait_send()
                corner_copy(c, k, near_at[k]).wait_send()
        elif n_group > 1:
            gone = xg.at[c, par, pl.ds(0, n_group - 1)]
            pltpu.make_async_copy(gone, gone, fsend.at[c, 0]).wait()
        share(c).wait_send()
    if n_blk > 1:
        gone = frames.at[pl.ds(0, n_blk - 1)]
        pltpu.make_async_copy(gone, gone, rsend).wait()

    @pl.loop(1, n_blk)
    def _(d):
        for way in range(2):
            @pl.when(can[way] & exists(way, d - 1))
            def _():
                for c in range(n_chunk):
                    line_copy(way, source(way, d - 1), d, c).wait_send()


def plane_kernel(
    dims,
    q_ref, tf_ref, x_ref, fr_ref, w_ref, qg_ref, kg_ref,
    out_ref,
    raw, kvw, xg, kv, frames, qv, qn, proj, outv, acc, tot,
    wsem, qsem, osem, lsem, nsend, nrecv, csend, crecv, ssend, srecv, xsend, xrecv,
    rsend, rrecv, zsend, zrecv, hsend, hrecv, ready,
):
    n_sec, n_blk, n_tp, sizes, n_early, n_extra = dims
    n_chunk = len(sizes)
    n_more = min(n_extra, 1)
    sizes = sizes + (sum(sizes[n_chunk - n_extra:]),)
    n_all = n_chunk + n_more
    first = [sum(sizes[:c]) for c in range(n_all)]
    sec, blk, tp = lax.axis_index("section"), lax.axis_index("blk"), lax.axis_index("tp")
    par = lax.rem(sec, 2)
    half = sec // 2
    rows, fw = x_ref.shape
    feats, _, kv_cols = w_ref.shape[1:]
    head = qg_ref.shape[1]
    heads_kv = kv_cols // head
    text = qv.shape[0]
    groups = qv.shape[1] // kv_cols
    n_slice = feats // fw
    last = n_blk - 1

    mine = half * n_tp + tp
    other = 2 * (1 - half) + par
    near = ({"section": other}, {"tp": 1 - tp})
    slots = (
        mine,
        (1 - half) * n_tp + tp,
        half * n_tp + 1 - tp,
        (1 - half) * n_tp + 1 - tp,
    )
    sibling = {"section": sec + 1 - 2 * par}

    x_copy = pltpu.make_async_copy(x_ref, xg.at[par, mine, pl.ds(0, rows)], lsem)

    def w_copy(i):
        span = pl.ds(i * fw, fw)
        return pltpu.make_async_copy(w_ref.at[0, span], raw.at[span], wsem.at[i])

    q_copy = pltpu.make_async_copy(q_ref, qv, qsem)
    x_copy.start()
    for i in range(n_slice):
        w_copy(i).start()
    q_copy.start()

    def line_peer(k):
        return {"blk": lax.rem(blk + k, n_blk)}

    def along(way):
        return blk if way == 0 else last - blk

    def at(way, u):
        return u if way == 0 else last - u

    barrier = pltpu.get_barrier_semaphore()
    for peer in (sibling, *near):
        pl.semaphore_signal(barrier, inc=1, device_id=peer, device_id_type=MESH)
    for way in range(2):
        @pl.when(along(way) < last)
        def _():
            ahead = {"blk": at(way, along(way) + 1)}
            pl.semaphore_signal(barrier, inc=1, device_id=ahead, device_id_type=MESH)

    inner = (blk > 0) & (blk < last)
    pl.semaphore_wait(barrier, 4 + inner.astype(jnp.int32))

    def tell(way, hops):
        ahead = {"blk": at(way, along(way) + 1)}
        pl.semaphore_signal(ready.at[way, hops], inc=1, device_id=ahead, device_id_type=MESH)

    def hear_far():
        for way in range(2):
            @pl.when(along(way) >= 2)
            def _():
                pl.semaphore_wait(ready.at[way, 0], 1)

            @pl.when(along(way) == 2)
            def _():
                tell(way, 1)

            @pl.when(along(way) == last)
            def _():
                pl.semaphore_wait(ready.at[way, 1], 1)

    def near_copy(c, k, slot):
        part = xg.at[par, slot, pl.ds(first[c], sizes[c])]
        return pltpu.make_async_remote_copy(
            src_ref=part,
            dst_ref=part,
            send_sem=nsend.at[c, k],
            recv_sem=nrecv.at[c, k],
            device_id=near[k],
            device_id_type=MESH,
        )

    def corner_copy(c, k, slot):
        part = xg.at[par, slot, pl.ds(first[c] + k * (sizes[c] // 2), sizes[c] // 2)]
        return pltpu.make_async_remote_copy(
            src_ref=part,
            dst_ref=part,
            send_sem=csend.at[c, k],
            recv_sem=crecv.at[c, k],
            device_id=near[1 - k],
            device_id_type=MESH,
        )

    def share(c, i, side):
        start, size = first[c], sizes[c]
        if i == 0 and c == 0:
            start, size = 0, rows
        part = xg.at[side, slots[i], pl.ds(start, size)]
        return pltpu.make_async_remote_copy(
            src_ref=part,
            dst_ref=part,
            send_sem=ssend.at[c, i],
            recv_sem=srecv.at[c, i],
            device_id=sibling,
            device_id_type=MESH,
        )

    def start(c):
        for k in range(2):
            near_copy(c, k, mine).start()
        if c == 0 or c >= n_chunk:
            share(c, 0, par).start()

    def forward(c):
        for k in range(2):
            near_copy(c, k, slots[k + 1]).wait_recv()
            corner_copy(c, k, slots[k + 1]).start()
            share(c, k + 1, par).start()

    def turn(c):
        for k in range(2):
            corner_copy(c, k, slots[3]).wait_recv()
        share(c, 3, par).start()

    at_end = (blk == 0) | (blk == last)

    def extra_copy(way, e):
        c = n_chunk - n_extra
        return pltpu.make_async_remote_copy(
            src_ref=xg.at[par, mine, pl.ds(first[c], sizes[n_chunk])],
            dst_ref=xg.at[par, mine, pl.ds(rows, sizes[n_chunk])],
            send_sem=xsend.at[e],
            recv_sem=xrecv.at[e],
            device_id={"blk": at(way, last)},
            device_id_type=MESH,
        )

    def start_extra():
        if n_extra > 0:
            @pl.when(at_end)
            def _():
                for e in range(n_more):
                    extra_copy(0, e).wait_recv()
                    start(n_chunk + e)

    def frame_copy(k):
        return pltpu.make_async_remote_copy(
            src_ref=fr_ref,
            dst_ref=frames.at[blk],
            send_sem=rsend,
            recv_sem=rrecv,
            device_id=line_peer(k),
            device_id_type=MESH,
        )

    x_copy.wait()
    start(0)
    start(1)
    for way in range(2):
        @pl.when(along(way) == 2)
        def _():
            for e in range(n_more):
                extra_copy(way, e).start()

    for way in range(2):
        @pl.when((along(way) >= 1) & (along(way) < last))
        def _():
            tell(way, 0)

    pltpu.make_async_copy(fr_ref, frames.at[blk], rrecv).start()

    part = fw // 2
    for i in range(n_slice):
        w_copy(i).wait()

        @pl.loop(0, fw // part, unroll=2)
        def _(j):
            span = pl.ds(pl.multiple_of(i * fw + j * part, part), part)
            kvw[span, :] = raw[span].reshape(part, 2 * kv_cols)

        if i == n_slice - 1:
            forward(0)
            start(2)

    hear_far()
    for k in range(1, n_blk):
        frame_copy(k).start()

    def line_copy(way, kind, src, to, c):
        piece = kv.at[src, :, pl.ds(first[c], sizes[c])]
        return pltpu.make_async_remote_copy(
            src_ref=piece,
            dst_ref=piece,
            send_sem=zsend.at[way, kind, c],
            recv_sem=zrecv.at[way, src, c],
            device_id={"blk": to},
            device_id_type=MESH,
        )

    def hop(way, c):
        return line_copy(way, 0, blk, at(way, along(way) + 1), c)

    def hops(way, c):
        return along(way) < (last if c < n_chunk - n_extra else 2)

    def relay_copy(way, d, c):
        u = along(way)
        return line_copy(way, d, at(way, u - d), at(way, u + 1), c)

    def head_copy(way, h):
        piece = kv.at[at(way, 0), h, pl.ds(first[n_early], rows - first[n_early])]
        return pltpu.make_async_remote_copy(
            src_ref=piece,
            dst_ref=piece,
            send_sem=hsend.at[way, h],
            recv_sem=hrecv.at[way, h],
            device_id={"blk": at(way, last)},
            device_id_type=MESH,
        )

    def arrived(way, u, c):
        line_copy(way, 0, at(way, u), blk, c).wait_recv()

    def send(c):
        for way in range(2):
            @pl.when(hops(way, c))
            def _():
                hop(way, c).start()

    def passes(way, d):
        return (along(way) >= d) & (along(way) < last)

    def relay(d, c):
        if d < 2 or c < n_early:
            for way in range(2):
                @pl.when(passes(way, d))
                def _():
                    arrived(way, along(way) - d, c)
                    relay_copy(way, d, c).start()

    def weight(p, slot):
        place = ((2 * (slot // n_tp) + p) * n_tp + lax.rem(slot, n_tp)) * fw
        return kvw[pl.ds(pl.multiple_of(place, fw), fw), :]

    proj[:rows, :] = jnp.dot(xg[par, mine, :rows, :], weight(par, mine), preferred_element_type=F32)
    share(0, 0, 1 - par).wait_recv()
    proj[:rows, :] += jnp.dot(xg[1 - par, mine, :rows, :], weight(1 - par, mine), preferred_element_type=F32)

    def add(c, i):
        span = slice(first[c], first[c] + sizes[c])
        for p in range(2):
            proj[span, :] += jnp.dot(
                xg[p, slots[i], span, :], weight(p, slots[i]), preferred_element_type=F32
            )

    def add_near(c):
        for i in (1, 2):
            share(c, i, 1 - par).wait_recv()
            add(c, i)

    def add_corner(c):
        share(c, 3, 1 - par).wait_recv()
        add(c, 3)

    def finish(c, src, to):
        span = slice(first[c], first[c] + sizes[c])
        for h in range(heads_kv):
            key = proj[span, h * head:(h + 1) * head]
            scale = lax.rsqrt(jnp.mean(key * key, axis=-1, keepdims=True) + EPS)
            kv[src, h, to:to + sizes[c], :head] = (key * scale * kg_ref[...]).astype(BF16)
            kv[src, h, to:to + sizes[c], head:] = (
                proj[span, kv_cols + h * head:kv_cols + (h + 1) * head].astype(BF16)
            )

    q_copy.wait()
    gain = qg_ref[...] * head ** (-0.5)

    @pl.loop(0, heads_kv)
    def _(k):
        for g in range(groups):
            col = pl.multiple_of((k * groups + g) * head, head)
            rowsq = qv[:, pl.ds(col, head)].astype(F32)
            scale = lax.rsqrt(jnp.mean(rowsq * rowsq, axis=-1, keepdims=True) + EPS)
            qn[k, g * text:(g + 1) * text, :] = (rowsq * scale * gain).astype(BF16)

    for c in range(n_chunk):
        add_near(c)
        if c + 1 < n_chunk:
            forward(c + 1)
            if c + 3 < n_chunk:
                start(c + 3)
            if c + 2 == n_chunk:
                start_extra()
        if c >= 2:
            relay(1, c - 2)
        if c >= 3:
            relay(2, c - 3)
        turn(c)
        add_corner(c)
        finish(c, blk, first[c])
        send(c)

    relay(1, n_chunk - 2)
    relay(2, n_chunk - 3)
    relay(1, n_chunk - 1)
    for c in range(n_chunk - 2, n_chunk):
        relay(2, c)

    for way in range(2):
        @pl.when(along(way) == 2)
        def _():
            for c in range(n_early, n_chunk):
                arrived(way, 0, c)
            for h in range(heads_kv):
                head_copy(way, h).start()

    if n_extra > 0:
        @pl.when(at_end)
        def _():
            beside = jnp.where(blk == 0, 1, last - 1)
            for c in range(n_chunk, n_all):
                span = slice(first[c], first[c] + sizes[c])
                proj[span, :] = jnp.zeros((sizes[c], proj.shape[1]), F32)
                share(c, 0, 1 - par).wait_recv()
                add(c, 0)
                forward(c)
                add_near(c)
                turn(c)
                add_corner(c)
                finish(c, beside, first[n_chunk - n_extra])

    pltpu.make_async_copy(frames, frames, rrecv).wait()
    limit = jnp.broadcast_to(tf_ref[...], (text, text)).T[:, :1]
    far = jnp.where(2 * blk < n_blk, last, 0)
    others = [jnp.where(far == 0, 1, 0) + i for i in range(n_blk - 1)]

    def part_of(k, blocks):
        keys = jnp.concatenate([kv[s, k, :, :head] for s in blocks], axis=0)
        values = jnp.concatenate([kv[s, k, :, head:] for s in blocks], axis=0)
        allowed = jnp.concatenate([frames[s] for s in blocks], axis=1) <= limit
        count = len(blocks) * rows
        scores = lax.dot_general(
            qn[k], keys, (((1,), (1,)), ((), ())), preferred_element_type=F32
        )
        weights = jnp.where(
            allowed[None], jnp.exp(scores).reshape(groups, text, count), 0.0
        ).reshape(groups * text, count)
        total = weights[:, :head]
        for m in range(1, count // head):
            total = total + weights[:, m * head:(m + 1) * head]
        return jnp.dot(weights.astype(BF16), values, preferred_element_type=F32), total

    for way in range(2):
        @pl.when(along(way) == last)
        def _():
            for c in range(n_chunk - n_extra):
                arrived(way, 2, c)
            for c in range(n_chunk):
                arrived(way, 1, c)

    def out_copy(k):
        return pltpu.make_async_copy(
            outv.at[k], out_ref.at[:, pl.ds(pl.multiple_of(k * groups * head, head), groups * head)], osem.at[k]
        )

    @pl.loop(0, heads_kv)
    def _(k):
        acc[k], tot[k] = part_of(k, others)

    for way in range(2):
        @pl.when(along(way) == last)
        def _():
            for c in range(n_early):
                arrived(way, 0, c)

    @pl.loop(0, heads_kv)
    def _(k):
        for way in range(2):
            @pl.when(along(way) == last)
            def _():
                head_copy(way, k).wait_recv()

        result, total = part_of(k, [far])
        total = jnp.sum(total + tot[k], axis=-1, keepdims=True)
        result = ((result + acc[k]) / total).astype(BF16)
        for g in range(groups):
            outv[k, :, g * head:(g + 1) * head] = result[g * text:(g + 1) * text]
        out_copy(k).start()

    def sent(c):
        for k in range(2):
            near_copy(c, k, mine).wait_send()
            corner_copy(c, k, slots[k + 1]).wait_send()
        for i in range(4):
            if i > 0 or c == 0 or c >= n_chunk:
                share(c, i, par).wait_send()

    for c in range(n_chunk):
        sent(c)
    if n_extra > 0:
        @pl.when(at_end)
        def _():
            for c in range(n_chunk, n_all):
                sent(c)

        @pl.when(jnp.logical_not(at_end))
        def _():
            for e in range(n_more):
                extra_copy(0, e).wait_send()

    gone = frames.at[pl.ds(0, n_blk - 1)]
    pltpu.make_async_copy(gone, gone, rsend).wait()
    for way in range(2):
        for c in range(n_chunk):
            @pl.when(hops(way, c))
            def _():
                hop(way, c).wait_send()

            @pl.when(passes(way, 1))
            def _():
                relay_copy(way, 1, c).wait_send()

            if c < n_early:
                @pl.when(passes(way, 2))
                def _():
                    relay_copy(way, 2, c).wait_send()

        @pl.when(along(way) == 2)
        def _():
            for h in range(heads_kv):
                head_copy(way, h).wait_send()

    @pl.loop(0, heads_kv)
    def _(k):
        out_copy(k).wait()


def solution(mesh):
    n_sec, n_blk, n_tp = mesh.shape["section"], mesh.shape["blk"], mesh.shape["tp"]

    def per_device(query, text_frame, image_feats, image_frame, kv_weight, query_gain, key_gain):
        text = query.shape[0]
        rows, fw = image_feats.shape
        feats, _, kv_cols = kv_weight.shape[1:]
        head = query_gain.shape[1]
        heads_kv = kv_cols // head
        groups = query.shape[1] // kv_cols
        n_chunk = 4
        rc = rows // n_chunk
        w_rows = 1024
        n_stage = 4
        n_group = n_sec // 2 * n_tp
        vmem = pl.BlockSpec(memory_space=pltpu.VMEM)
        dma = pltpu.SemaphoreType.DMA
        if n_sec == 4 and n_blk == 4 and n_tp == 2 and rows % 128 == 0:
            sizes = tuple(rows * part // 8 for part in PARTS)
            n_part = len(sizes)
            n_all = n_part + 1
            taller = rows + sum(sizes[n_part - EXTRA:])
            anywhere = pl.BlockSpec(memory_space=pl.ANY)
            return pl.pallas_call(
                functools.partial(plane_kernel, (n_sec, n_blk, n_tp, sizes, EARLY, EXTRA)),
                out_shape=jax.ShapeDtypeStruct(query.shape, BF16),
                in_specs=[anywhere, vmem, anywhere, vmem, anywhere, vmem, vmem],
                out_specs=anywhere,
                scratch_shapes=[
                    pltpu.VMEM((feats, 2, kv_cols), BF16),
                    pltpu.VMEM((feats, 2 * kv_cols), BF16),
                    pltpu.VMEM((2, n_group, taller, fw), BF16),
                    pltpu.VMEM((n_blk, heads_kv, rows, 2 * head), BF16),
                    pltpu.VMEM((n_blk, 1, rows), jnp.int32),
                    pltpu.VMEM(query.shape, BF16),
                    pltpu.VMEM((heads_kv, groups * text, head), BF16),
                    pltpu.VMEM((taller, 2 * kv_cols), F32),
                    pltpu.VMEM((heads_kv, text, groups * head), BF16),
                    pltpu.VMEM((heads_kv, groups * text, head), F32),
                    pltpu.VMEM((heads_kv, groups * text, head), F32),
                    dma((feats // fw,)),
                    dma,
                    dma((heads_kv,)),
                    dma,
                    dma((n_all, 2)),
                    dma((n_all, 2)),
                    dma((n_all, 2)),
                    dma((n_all, 2)),
                    dma((n_all, 4)),
                    dma((n_all, 4)),
                    dma((max(EXTRA, 1),)),
                    dma((max(EXTRA, 1),)),
                    dma,
                    dma,
                    dma((2, 4, n_part)),
                    dma((2, n_blk, n_part)),
                    dma((2, heads_kv)),
                    dma((2, heads_kv)),
                    pltpu.SemaphoreType.REGULAR((2, 2)),
                ],
                compiler_params=pltpu.CompilerParams(
                    collective_id=1, has_side_effects=True, vmem_limit_bytes=58 << 20
                ),
            )(
                query,
                text_frame.reshape(1, text),
                image_feats,
                image_frame.reshape(1, rows),
                kv_weight,
                query_gain,
                key_gain,
            )
        return pl.pallas_call(
            functools.partial(kernel, (n_sec, n_blk, n_tp, n_chunk, w_rows)),
            out_shape=jax.ShapeDtypeStruct(query.shape, BF16),
            in_specs=[vmem, vmem, vmem, vmem, pl.BlockSpec(memory_space=pl.ANY), vmem, vmem],
            out_specs=vmem,
            scratch_shapes=[
                pltpu.VMEM((n_stage, w_rows, 2, kv_cols), BF16),
                pltpu.VMEM((feats, 2 * kv_cols), BF16),
                pltpu.VMEM((n_chunk, 2, n_group, rc, fw), BF16),
                pltpu.VMEM((n_blk, n_chunk, rc, 2 * kv_cols), BF16),
                pltpu.VMEM((n_blk, 1, rows), jnp.int32),
                pltpu.VMEM((heads_kv, groups * text, head), BF16),
                pltpu.VMEM((heads_kv, groups * text, head), F32),
                pltpu.VMEM((heads_kv, groups * text, head), F32),
                pltpu.VMEM((rc, 2 * kv_cols), F32),
                dma((n_stage,)),
                dma((n_chunk, 4)),
                dma((n_chunk, 5)),
                dma((n_chunk,)),
                dma((n_chunk,)),
                dma,
                dma,
                dma((2, n_blk, n_chunk)),
                dma((2, n_blk, n_chunk)),
            ],
            compiler_params=pltpu.CompilerParams(
                collective_id=0, has_side_effects=True, vmem_limit_bytes=56 << 20
            ),
        )(
            query,
            text_frame.reshape(1, text),
            image_feats,
            image_frame.reshape(1, rows),
            kv_weight,
            query_gain,
            key_gain,
        )

    return jax.shard_map(
        per_device,
        mesh=mesh,
        in_specs=(
            P(("section", "blk"), "tp"),
            P(("section", "blk")),
            P("blk", ("section", "tp")),
            P("blk"),
            P("section", None, None, "tp"),
            P("section", None),
            P("section", None),
        ),
        out_specs=P(("section", "blk"), "tp"),
        check_vma=False,
    )
```
